32 devices in a mesh: groups: 2 (over x), tile: 16 (over z, y, core).
Axes of the slice: x: 2, y: 2, z: 4, core: 2. Of those that a mesh axis runs over, the one named last changes fastest.
Arguments:
- start_model: float32 [2, 32768, 128], P(None, ('groups', 'tile')), parts along dimension 1, may hold values from -6 to 6
- v_basis: bfloat16 [2, 26624, 1024], P(None, ('groups', 'tile')), parts along dimension 1, may hold values from -0.125 to 0.125
- u_basis: bfloat16 [2, 1, 832, 32768], P(None, None, None, ('groups', 'tile')), parts along dimension 3, may hold values from -0.15625 to 0.15625
- records: bfloat16 [32, 128, 32768], P(None, None, ('groups', 'tile')), parts along dimension 2, may hold values from -6 to 6
- tile_ranks: int32 [2, 16, 16], P('groups'), parts along dimension 0, may hold values from 8 to 96, as said below
- window_start: int32 [128, 32768], P(None, ('groups', 'tile')), parts along dimension 1, may hold values from 0 to 7, as said below
- window_stop: int32 [128, 32768], P(None, ('groups', 'tile')), parts along dimension 1, may hold values from 16 to 31
Outputs:
- final_model: float32 [2, 32768, 128], P(None, ('groups', 'tile')), parts along dimension 1
The draws below stay inside these ranges and needn't reach their ends.
There are 2 independent parts, one for each index of `groups`. The reference program is written for one: setup_inputs(seed, part) draws one part's arguments, and reference() takes and returns one part's arrays. A program takes and returns all parts, laid end to end along the dimension named above; each array names one. Nothing has to cross between parts.
Inputs may be any that keep to these rules, and one draw needn't show every extreme that they name: `tile_ranks`: every tile row and every tile column of one frequency holds the same 16 ranks, each once, and they sum to 832; every frequency has tiles of rank 96 and of rank 8. window_stop - window_start lies between 16 and 24 for every pair.
All inputs are finite; a program needn't handle non-finite values.
Results may differ from the reference program's by a relative error of at most 0.012.
Values may be sent and summed in bfloat16 or wider, within the bound.
A program may use at most 128 MiB of HBM per device.

```python
import math
import jax
import jax.numpy as jnp
from jax import lax

NB = 1024
CT = 16
RT = 16
NVS = 128
RMIN = 8
RMAX = 96
NT = 32
ITERS = 2
F = 1
N = 16384
NR = 16384
RSUM = 832
PIECES = 1
PROWS = 1024


def permute_tiles(subkey):
    return jax.random.permutation(subkey, CT).astype(jnp.int32)


def rank_layout(key):
    half_count = CT // 2
    chosen = jax.random.randint(jax.random.fold_in(key, 11), (F, half_count), RMIN, RMAX + 1)
    leading = jnp.arange(half_count, dtype=jnp.int32)[None, :] == 0
    chosen = jnp.where(leading, RMAX, chosen)
    rank_values = jnp.concatenate([chosen, RMIN + RMAX - chosen], axis=1)
    row_keys = jax.random.split(jax.random.fold_in(key, 12), F)
    col_keys = jax.random.split(jax.random.fold_in(key, 13), F)
    row_order = jax.vmap(permute_tiles)(row_keys)
    col_order = jax.vmap(permute_tiles)(col_keys)
    position = (row_order[:, :, None] + col_order[:, None, :]) % CT
    spread = jnp.broadcast_to(rank_values[:, None, :], (F, RT, CT))
    return jnp.take_along_axis(spread, position, axis=2).astype(jnp.int32)


def window_layout(key):
    openings = jax.random.randint(jax.random.fold_in(key, 21), (NVS, NR), 0, NT // 4)
    spans = jax.random.randint(jax.random.fold_in(key, 22), (NVS, NR), NT // 2, 3 * NT // 4 + 1)
    return (openings.astype(jnp.int32), (openings + spans).astype(jnp.int32))


def draw_tile_ranks(key, part):
    return rank_layout(key)


def draw_window_start(key, part):
    return window_layout(key)[0]


def draw_window_stop(key, part):
    return window_layout(key)[1]


def block_levels(stream_key, shape, pieces, low, top_value):
    level = 1.0
    for dim, parts in pieces:
        heights = jax.random.uniform(jax.random.fold_in(jax.random.fold_in(stream_key, 6), dim), (parts,), jnp.float32, low / len(pieces), top_value / len(pieces))
        level = level * jnp.repeat(jnp.exp(heights), shape[dim] // parts).reshape((-1,) + (1,) * (len(shape) - 1 - dim))
    return level


def scatter_about(stream_key, extent, scale, reach, cuts=(), kind=jnp.bfloat16):
    factor_of = block_levels(stream_key, extent, cuts, -0.22, 0.18) if cuts else 1.0
    values = jax.random.normal(stream_key, extent, jnp.float32) * scale * factor_of
    return jnp.minimum(jnp.maximum(values, -reach), reach).astype(kind)


def setup_inputs(seed: int = 0, part: int = 0) -> dict:
    streams_of = jax.random.split(jax.random.key(seed), 8)
    own_keys = jax.random.split(jax.random.fold_in(streams_of[7], part), 8)
    start_model = scatter_about(own_keys[0], (2, F * N, NVS), 1.0, 6.0, ((1, 16),), jnp.float32)
    v_basis = scatter_about(own_keys[1], (2, F * CT * RSUM, NB), (2 * NB) ** -0.5, 0.125, ((1, 16),))
    u_basis = scatter_about(own_keys[2], (2, F, RSUM, NR), (2 * RSUM) ** -0.5, 0.15625, ((3, 16),))
    records = scatter_about(own_keys[3], (NT, NVS, NR), 1.0, 6.0, ((2, 16),))
    tile_ranks = draw_tile_ranks(jax.random.fold_in(jax.random.fold_in(streams_of[7], part), 71), part)
    window_start = draw_window_start(jax.random.fold_in(jax.random.fold_in(streams_of[7], part), 71), part)
    window_stop = draw_window_stop(jax.random.fold_in(jax.random.fold_in(streams_of[7], part), 71), part)
    return dict(start_model=start_model, v_basis=v_basis, u_basis=u_basis, records=records, tile_ranks=tile_ranks, window_start=window_start, window_stop=window_stop)


step_size = 0.5
precise = lax.Precision.HIGHEST

def wave_tables(bin_count, sample_count):
    moments = jnp.arange(sample_count, dtype=jnp.float32)
    bin_ids = jnp.arange(bin_count, dtype=jnp.float32) + 1.0
    phases = 2.0 * math.pi / sample_count * bin_ids[:, None] * moments[None, :]
    factor = math.sqrt(2.0 / sample_count)
    return (jnp.cos(phases) * factor, jnp.sin(phases) * factor)

def unpack_index(starts, slot_total):
    slot_ids = jnp.arange(slot_total, dtype=jnp.int32)
    owners = lax.optimization_barrier(jnp.sum((starts[..., None, :] <= slot_ids[:, None]).astype(jnp.int32), axis=-1)) - 1
    owner_start = jnp.take_along_axis(starts, owners, axis=-1)
    return (owners, slot_ids - owner_start)

def piece_tree(partials, axis):
    current = partials
    while current.shape[axis] > 1:
        half_count = current.shape[axis] // 2
        lower_part = lax.slice_in_dim(current, 0, half_count, axis=axis).astype(jnp.float32)
        upper_part = lax.slice_in_dim(current, half_count, 2 * half_count, axis=axis).astype(jnp.float32)
        current = lax.optimization_barrier((lower_part + upper_part).astype(jnp.bfloat16))
    return jnp.squeeze(current, axis)

def reference(start_model, v_basis, u_basis, records, tile_ranks, window_start, window_stop):
    down_offsets = jnp.cumsum(tile_ranks, axis=1) - tile_ranks
    side_offsets = jnp.cumsum(tile_ranks, axis=2) - tile_ranks
    col_owner, col_slot = unpack_index(side_offsets, RSUM)
    gather_u = (col_owner * RSUM + jnp.take_along_axis(down_offsets, col_owner, axis=2) + col_slot).astype(jnp.int32)
    down_swap = jnp.transpose(down_offsets, (0, 2, 1))
    side_swap = jnp.transpose(side_offsets, (0, 2, 1))
    row_owner, row_slot = unpack_index(down_swap, RSUM)
    gather_v = (row_owner * RSUM + jnp.take_along_axis(side_swap, row_owner, axis=2) + row_slot).astype(jnp.int32)
    v_blocks = jnp.transpose(v_basis.reshape(2, F, CT, RSUM, NB), (1, 0, 2, 3, 4))
    u_blocks = jnp.transpose(u_basis, (1, 0, 2, 3))
    cos_table, sin_table = wave_tables(F, NT)

    def forward_one(operands):
        v_freq, x_freq, u_freq, gather_ids = operands
        v_wide = v_freq.astype(jnp.float32)
        coeff_real = jnp.einsum('jkn,jns->jks', v_wide[0], x_freq[0]) - jnp.einsum('jkn,jns->jks', v_wide[1], x_freq[1])
        coeff_imag = jnp.einsum('jkn,jns->jks', v_wide[0], x_freq[1]) + jnp.einsum('jkn,jns->jks', v_wide[1], x_freq[0])
        packed = lax.optimization_barrier(jnp.stack([coeff_real, coeff_imag]).astype(jnp.bfloat16))
        packed = packed.astype(jnp.float32).reshape(2, CT * RSUM, NVS)
        chosen = packed[:, gather_ids]
        u_wide = u_freq.astype(jnp.float32).reshape(2, RSUM, RT, NB)
        pred_real = jnp.einsum('iks,kin->sin', chosen[0], u_wide[0]) - jnp.einsum('iks,kin->sin', chosen[1], u_wide[1])
        pred_imag = jnp.einsum('iks,kin->sin', chosen[0], u_wide[1]) + jnp.einsum('iks,kin->sin', chosen[1], u_wide[0])
        return jnp.stack([pred_real, pred_imag]).reshape(2, NVS, NR)

    def misfit_block(operands):
        pred_block, record_block, open_block, close_block = operands
        traces = jnp.einsum('ft,fsn->tsn', cos_table, pred_block[:, 0], precision=precise) - jnp.einsum('ft,fsn->tsn', sin_table, pred_block[:, 1], precision=precise)
        moments = jnp.arange(NT, dtype=jnp.int32)[:, None, None]
        inside = (moments >= open_block[None]) & (moments < close_block[None])
        residual = jnp.where(inside, traces - record_block.astype(jnp.float32), jnp.zeros((), jnp.float32))
        back_real = jnp.einsum('ft,tsn->fsn', cos_table, residual, precision=precise)
        back_imag = -jnp.einsum('ft,tsn->fsn', sin_table, residual, precision=precise)
        return jnp.stack([back_real, back_imag], axis=1).astype(jnp.bfloat16)

    def adjoint_one(operands):
        u_freq, back_freq, v_freq, gather_ids = operands
        u_wide = u_freq.astype(jnp.float32).reshape(2, RSUM, RT, PIECES, PROWS)
        back_wide = back_freq.astype(jnp.float32).reshape(2, NVS, RT, PIECES, PROWS)
        part_real = jnp.einsum('kipn,sipn->ipks', u_wide[0], back_wide[0]) + jnp.einsum('kipn,sipn->ipks', u_wide[1], back_wide[1])
        part_imag = jnp.einsum('kipn,sipn->ipks', u_wide[0], back_wide[1]) - jnp.einsum('kipn,sipn->ipks', u_wide[1], back_wide[0])
        partials = lax.optimization_barrier(jnp.stack([part_real, part_imag]).astype(jnp.bfloat16))
        summed = piece_tree(partials, 2)
        summed = summed.astype(jnp.float32).reshape(2, RT * RSUM, NVS)
        chosen = summed[:, gather_ids]
        v_wide = v_freq.astype(jnp.float32)
        grad_real = jnp.einsum('jkn,jks->jns', v_wide[0], chosen[0]) + jnp.einsum('jkn,jks->jns', v_wide[1], chosen[1])
        grad_imag = jnp.einsum('jkn,jks->jns', v_wide[0], chosen[1]) - jnp.einsum('jkn,jks->jns', v_wide[1], chosen[0])
        return jnp.stack([grad_real, grad_imag])
    record_blocks = jnp.transpose(records.reshape(NT, NVS, RT, NB), (2, 0, 1, 3))
    open_blocks = jnp.transpose(window_start.reshape(NVS, RT, NB), (1, 0, 2))
    close_blocks = jnp.transpose(window_stop.reshape(NVS, RT, NB), (1, 0, 2))
    current = start_model
    for iteration in range(ITERS):
        rounded = lax.optimization_barrier(current.astype(jnp.bfloat16)).astype(jnp.float32)
        x_blocks = jnp.transpose(rounded.reshape(2, F, CT, NB, NVS), (1, 0, 2, 3, 4))
        predicted = lax.map(forward_one, (v_blocks, x_blocks, u_blocks, gather_u))
        pred_blocks = jnp.transpose(predicted.reshape(F, 2, NVS, RT, NB), (3, 0, 1, 2, 4))
        back_blocks = lax.map(misfit_block, (pred_blocks, record_blocks, open_blocks, close_blocks))
        backward = jnp.transpose(back_blocks, (1, 2, 3, 0, 4)).reshape(F, 2, NVS, NR)
        gradient = lax.map(adjoint_one, (u_blocks, backward, v_blocks, gather_v))
        gradient = jnp.transpose(gradient, (1, 0, 2, 3, 4)).reshape(2, F * N, NVS)
        current = current - step_size * gradient
    return current
```

```python
import functools
import math

import jax
import jax.numpy as jnp
from jax import lax
from jax.experimental import pallas as pl
from jax.experimental.pallas import tpu as pltpu
from jax.sharding import PartitionSpec as P

RMAX = 96
ITERS = 2
USE_KERNEL = True


step_size = 0.5
precise = lax.Precision.HIGHEST


def wave_tables(bin_count, sample_count):
    moments = jnp.arange(sample_count, dtype=jnp.float32)
    bin_ids = jnp.arange(bin_count, dtype=jnp.float32) + 1.0
    phases = 2.0 * math.pi / sample_count * bin_ids[:, None] * moments[None, :]
    factor = math.sqrt(2.0 / sample_count)
    return (jnp.cos(phases) * factor, jnp.sin(phases) * factor)


def unpack_index(starts, slot_total):
    slot_ids = jnp.arange(slot_total, dtype=jnp.int32)
    owners = jnp.sum((starts[..., None, :] <= slot_ids[:, None]).astype(jnp.int32), axis=-1) - 1
    owner_start = jnp.take_along_axis(starts, owners, axis=-1)
    return (owners, slot_ids - owner_start)


def piece_tree(partials, axis):
    current = partials
    while current.shape[axis] > 1:
        half_count = current.shape[axis] // 2
        lower_part = lax.slice_in_dim(current, 0, half_count, axis=axis).astype(jnp.float32)
        upper_part = lax.slice_in_dim(current, half_count, 2 * half_count, axis=axis).astype(
            jnp.float32
        )
        current = (lower_part + upper_part).astype(jnp.bfloat16)
    return jnp.squeeze(current, axis)


def pick_rows(source_rows, row_index):
    return source_rows[:, row_index]


def pack_slots(source_rows, rank_each, start_each, slot_pos):
    live_slots = slot_pos < rank_each[:, None]
    row_index = jnp.minimum(start_each[:, None] + slot_pos, source_rows.shape[1] - 1)
    return jnp.where(
        live_slots[None, :, :, None], source_rows[:, row_index], jnp.zeros((), source_rows.dtype)
    )


def on_device_general(start_model, v_basis, u_basis, records, tile_ranks, window_start, window_stop):
    tile_count = lax.axis_size("tile")
    device = lax.axis_index("tile")
    freq_count, rows_count, cols_count = tile_ranks.shape
    rank_total = v_basis.shape[1]
    pieces = tile_count // rows_count
    my_freq = device // cols_count
    my_col = device % cols_count
    my_row = device // pieces
    down_offsets = jnp.cumsum(tile_ranks, axis=1) - tile_ranks
    side_offsets = jnp.cumsum(tile_ranks, axis=2) - tile_ranks
    column_ranks = lax.dynamic_index_in_dim(
        lax.dynamic_index_in_dim(tile_ranks, my_freq, 0, False), my_col, 1, False
    )
    column_starts = lax.dynamic_index_in_dim(
        lax.dynamic_index_in_dim(down_offsets, my_freq, 0, False), my_col, 1, False
    )
    row_ranks = lax.dynamic_index_in_dim(tile_ranks, my_row, 1, False)
    row_starts = lax.dynamic_index_in_dim(side_offsets, my_row, 1, False)
    col_owner, col_slot = unpack_index(row_starts, rank_total)
    gather_u = col_owner * RMAX + col_slot
    row_owner, row_slot = unpack_index(column_starts, rank_total)
    gather_v = row_owner * RMAX + row_slot
    fwd_rank = jnp.broadcast_to(column_ranks[:, None], (rows_count, pieces)).reshape(tile_count)
    fwd_start = jnp.broadcast_to(column_starts[:, None], (rows_count, pieces)).reshape(tile_count)
    dest_freq = jnp.arange(tile_count, dtype=jnp.int32) // cols_count
    adj_rank = row_ranks.reshape(tile_count)
    adj_start = row_starts.reshape(tile_count) + dest_freq * rank_total
    full_slots = jnp.broadcast_to(jnp.arange(RMAX, dtype=jnp.int32)[None, :], (tile_count, RMAX))
    cos_table, sin_table = wave_tables(freq_count, records.shape[0])
    moments = jnp.arange(records.shape[0], dtype=jnp.int32)[:, None, None]
    inside = (moments >= window_start[None]) & (moments < window_stop[None])
    observed = records.astype(jnp.float32)
    current = start_model
    for iteration in range(ITERS):
        rounded = current.astype(jnp.bfloat16)
        coeff_real = jnp.dot(v_basis[0], rounded[0], preferred_element_type=jnp.float32) - jnp.dot(
            v_basis[1], rounded[1], preferred_element_type=jnp.float32
        )
        coeff_imag = jnp.dot(v_basis[0], rounded[1], preferred_element_type=jnp.float32) + jnp.dot(
            v_basis[1], rounded[0], preferred_element_type=jnp.float32
        )
        coefficients = jnp.stack([coeff_real, coeff_imag]).astype(jnp.bfloat16)
        outbound = pack_slots(coefficients, fwd_rank, fwd_start, full_slots)
        forward_received = lax.all_to_all(outbound, "tile", split_axis=1, concat_axis=1, tiled=True)
        flattened = forward_received.reshape(2, freq_count, -1, forward_received.shape[3])
        forward_chosen = jax.vmap(pick_rows, in_axes=(1, 0), out_axes=1)(flattened, gather_u)
        pred_real = jnp.einsum(
            "fks,fkn->fsn", forward_chosen[0], u_basis[0], preferred_element_type=jnp.float32
        ) - jnp.einsum(
            "fks,fkn->fsn", forward_chosen[1], u_basis[1], preferred_element_type=jnp.float32
        )
        pred_imag = jnp.einsum(
            "fks,fkn->fsn", forward_chosen[0], u_basis[1], preferred_element_type=jnp.float32
        ) + jnp.einsum(
            "fks,fkn->fsn", forward_chosen[1], u_basis[0], preferred_element_type=jnp.float32
        )
        predicted = jnp.stack([pred_real, pred_imag])
        traces = jnp.einsum("ft,fsn->tsn", cos_table, predicted[0], precision=precise) - jnp.einsum(
            "ft,fsn->tsn", sin_table, predicted[1], precision=precise
        )
        residual = jnp.where(inside, traces - observed, jnp.zeros((), jnp.float32))
        back_real = jnp.einsum("ft,tsn->fsn", cos_table, residual, precision=precise)
        back_imag = -jnp.einsum("ft,tsn->fsn", sin_table, residual, precision=precise)
        adjoint_field = jnp.stack([back_real, back_imag]).astype(jnp.bfloat16)
        part_real = jnp.einsum(
            "fkn,fsn->fks", u_basis[0], adjoint_field[0], preferred_element_type=jnp.float32
        ) + jnp.einsum(
            "fkn,fsn->fks", u_basis[1], adjoint_field[1], preferred_element_type=jnp.float32
        )
        part_imag = jnp.einsum(
            "fkn,fsn->fks", u_basis[0], adjoint_field[1], preferred_element_type=jnp.float32
        ) - jnp.einsum(
            "fkn,fsn->fks", u_basis[1], adjoint_field[0], preferred_element_type=jnp.float32
        )
        partial_value = jnp.stack([part_real, part_imag]).astype(jnp.bfloat16)
        flat_partial = partial_value.reshape(2, freq_count * rank_total, partial_value.shape[3])
        outgoing = pack_slots(flat_partial, adj_rank, adj_start, full_slots)
        received = lax.all_to_all(outgoing, "tile", split_axis=1, concat_axis=1, tiled=True)
        grouped_rows = received.reshape(2, rows_count, pieces, RMAX, received.shape[3])
        adjoint_summed = piece_tree(grouped_rows, 2)
        chosen = adjoint_summed.reshape(2, rows_count * RMAX, received.shape[3])[:, gather_v]
        contract_dims = (((0,), (0,)), ((), ()))
        grad_real = lax.dot_general(
            v_basis[0], chosen[0], contract_dims, preferred_element_type=jnp.float32
        ) + lax.dot_general(
            v_basis[1], chosen[1], contract_dims, preferred_element_type=jnp.float32
        )
        grad_imag = lax.dot_general(
            v_basis[0], chosen[1], contract_dims, preferred_element_type=jnp.float32
        ) - lax.dot_general(
            v_basis[1], chosen[0], contract_dims, preferred_element_type=jnp.float32
        )
        gradient = jnp.stack([grad_real, grad_imag])
        current = current - step_size * gradient
    return current


LANES = 128
VMEM_GRANT = 40 * 1024 * 1024
f32 = jnp.float32
bf16 = jnp.bfloat16
on_chip = pl.BlockSpec(memory_space=pltpu.VMEM)
scalars = pl.BlockSpec(memory_space=pltpu.SMEM)


def window_kernel(record_ref, open_ref, close_ref, out_ref):
    sample_count = record_ref.shape[0]
    scale = math.sqrt(2.0 / sample_count)
    opened = open_ref[...]
    closed = close_ref[...]
    zero = jnp.zeros(opened.shape, f32)
    sums = [zero] * 5
    for t in range(sample_count):
        phase = 2.0 * math.pi / sample_count * t
        c, s = math.cos(phase) * scale, math.sin(phase) * scale
        inside = (t >= opened) & (t < closed)
        one = jnp.where(inside, 1.0, 0.0)
        seen = jnp.where(inside, record_ref[t].astype(f32), 0.0)
        terms = [one * (c * c), one * (c * s), one * (s * s), seen * c, seen * s]
        sums = [a + b for a, b in zip(sums, terms)]
    for k in range(5):
        out_ref[k] = sums[k]


def window_sums(records, window_start, window_stop):
    samples, sources, receivers = records.shape
    rows = 8
    return pl.pallas_call(
        window_kernel,
        grid=(sources // rows,),
        in_specs=[
            pl.BlockSpec((samples, rows, receivers), lambda i: (0, i, 0)),
            pl.BlockSpec((rows, receivers), lambda i: (i, 0)),
            pl.BlockSpec((rows, receivers), lambda i: (i, 0)),
        ],
        out_specs=pl.BlockSpec((5, rows, receivers), lambda i: (0, i, 0)),
        out_shape=jax.ShapeDtypeStruct((5, sources, receivers), f32),
        compiler_params=pltpu.CompilerParams(vmem_limit_bytes=16 * 1024 * 1024),
        cost_estimate=pl.CostEstimate(
            flops=12 * samples * sources * receivers,
            bytes_accessed=2 * samples * sources * receivers,
            transcendentals=0,
        ),
    )(records, window_start, window_stop)


def starts_of(count, rank_at):
    starts, total = [], 0
    for k in range(count):
        starts.append(total)
        total = total + rank_at(k)
    return starts


def pack(rows_ref, starts, out_ref):
    for k, start in enumerate(starts):
        for part in range(2):
            lanes = pl.ds(part * LANES, LANES)
            out_ref[k, :, lanes] = rows_ref[part, pl.ds(start, RMAX), :].astype(bf16)


def unpack(slots_ref, starts, rows_ref):
    for k, start in enumerate(starts):
        for part in range(2):
            lanes = pl.ds(part * LANES, LANES)
            rows_ref[part, pl.ds(start, RMAX), :] = slots_ref[k, :, lanes].astype(f32)


def packed_rows(rows_ref, total):
    parts = [rows_ref[part, :total, :].astype(bf16) for part in range(2)]
    return jnp.concatenate(parts, axis=1)


def dot_last(a, b):
    return lax.dot_general(a, b, (((1,), (1,)), ((), ())), preferred_element_type=f32)


def dot_first(a, b):
    return lax.dot_general(a, b, (((0,), (0,)), ((), ())), preferred_element_type=f32)


def forward_rows(v_ref, xt, rows_ref):
    half = xt.shape[0] // 2
    total = v_ref.shape[1]
    xb = xt.astype(bf16)
    p = dot_last(v_ref[0], xb)
    q = dot_last(v_ref[1], xb)
    rows_ref[0, :total, :] = p[:, :half] - q[:, half:]
    rows_ref[1, :total, :] = p[:, half:] + q[:, :half]
    spare = rows_ref.shape[1] - total
    rows_ref[:, total:, :] = jnp.zeros((2, spare, half), f32)


def first_kernel(rank_ref, x_ref, v_ref, xt_ref, out_ref, rows_ref):
    me = lax.axis_index("tile")
    half = x_ref.shape[2]
    xt_ref[:half] = x_ref[0].T
    xt_ref[half:] = x_ref[1].T
    forward_rows(v_ref, xt_ref[...], rows_ref)
    count = rank_ref.shape[0]
    pack(rows_ref, starts_of(count, lambda k: rank_ref[k, me]), out_ref)


def data_kernel(rank_ref, slots_ref, u_ref, sums_ref, out_ref, rows_ref):
    me = lax.axis_index("tile")
    count = rank_ref.shape[1]
    total = u_ref.shape[1]
    half = sums_ref.shape[1]
    starts = starts_of(count, lambda k: rank_ref[me, k])
    unpack(slots_ref, starts, rows_ref)
    c = packed_rows(rows_ref, total)
    p = dot_first(c, u_ref[0])
    q = dot_first(c, u_ref[1])
    yr = p[:half] - q[half:]
    yi = q[:half] + p[half:]
    hr = sums_ref[0] * yr - sums_ref[1] * yi - sums_ref[3]
    hi = sums_ref[2] * yi - sums_ref[1] * yr + sums_ref[4]
    h = jnp.concatenate([hr, hi], axis=0).astype(bf16)
    p = dot_last(u_ref[0], h)
    q = dot_last(u_ref[1], h)
    rows_ref[0, :total, :] = p[:, :half] + q[:, half:]
    rows_ref[1, :total, :] = p[:, half:] - q[:, :half]
    pack(rows_ref, starts, out_ref)


def gradient_of(rank_ref, slots_ref, v_ref, xt_ref, rows_ref):
    me = lax.axis_index("tile")
    count = rank_ref.shape[0]
    total = v_ref.shape[1]
    half = xt_ref.shape[0] // 2
    starts = starts_of(count, lambda k: rank_ref[k, me])
    unpack(slots_ref, starts, rows_ref)
    a = packed_rows(rows_ref, total)
    p = dot_first(a, v_ref[0])
    q = dot_first(a, v_ref[1])
    xr = xt_ref[:half] - step_size * (p[:half] + q[half:])
    xi = xt_ref[half:] - step_size * (p[half:] - q[:half])
    return starts, xr, xi


def model_kernel(rank_ref, slots_ref, v_ref, xt_ref, new_ref, out_ref, rows_ref):
    half = xt_ref.shape[0] // 2
    starts, xr, xi = gradient_of(rank_ref, slots_ref, v_ref, xt_ref, rows_ref)
    new_ref[:half] = xr
    new_ref[half:] = xi
    forward_rows(v_ref, new_ref[...], rows_ref)
    pack(rows_ref, starts, out_ref)


def last_kernel(rank_ref, slots_ref, v_ref, xt_ref, out_ref, rows_ref):
    starts, xr, xi = gradient_of(rank_ref, slots_ref, v_ref, xt_ref, rows_ref)
    out_ref[0] = xr.T
    out_ref[1] = xi.T


def exchange_kernel(n, send_ref, recv_ref, send_sem, recv_sem, own_sem):
    me = lax.axis_index("tile")
    peers = [lax.rem(me + d, n) for d in range(1, n)]
    barrier = pltpu.get_barrier_semaphore()
    for peer in peers:
        pl.semaphore_signal(
            barrier, inc=1, device_id={"tile": peer}, device_id_type=pl.DeviceIdType.MESH
        )
    own = pltpu.make_async_copy(send_ref.at[me], recv_ref.at[me], own_sem)
    own.start()
    pl.semaphore_wait(barrier, n - 1)
    copies = []
    for d, peer in enumerate(peers):
        copy = pltpu.make_async_remote_copy(
            src_ref=send_ref.at[peer],
            dst_ref=recv_ref.at[me],
            send_sem=send_sem.at[d],
            recv_sem=recv_sem.at[d],
            device_id={"tile": peer},
            device_id_type=pl.DeviceIdType.MESH,
        )
        copy.start()
        copies.append(copy)
    own.wait()
    for copy in copies:
        copy.wait()


def exchange(slots):
    if not USE_KERNEL:
        return lax.all_to_all(slots, "tile", split_axis=0, concat_axis=0, tiled=True)
    n = slots.shape[0]
    return pl.pallas_call(
        functools.partial(exchange_kernel, n),
        out_shape=jax.ShapeDtypeStruct(slots.shape, slots.dtype),
        in_specs=[on_chip],
        out_specs=on_chip,
        scratch_shapes=[
            pltpu.SemaphoreType.DMA((n - 1,)),
            pltpu.SemaphoreType.DMA((n - 1,)),
            pltpu.SemaphoreType.DMA,
        ],
        compiler_params=pltpu.CompilerParams(
            collective_id=0, has_side_effects=True, vmem_limit_bytes=8 * 1024 * 1024
        ),
    )(slots)


def on_device(start_model, v_basis, u_basis, records, tile_ranks, window_start, window_stop):
    n = lax.axis_size("tile")
    freq_count, rows_count, cols_count = tile_ranks.shape
    single = freq_count == 1 and n == rows_count and n == cols_count
    if not single or start_model.shape[2] != LANES:
        return on_device_general(
            start_model, v_basis, u_basis, records, tile_ranks, window_start, window_stop
        )
    _, model_rows, sources = start_model.shape
    total = v_basis.shape[1]
    ranks = tile_ranks[0]
    u_parts = u_basis[:, 0]
    rows = [pltpu.VMEM((2, total + RMAX, sources), f32)]
    slots_like = jax.ShapeDtypeStruct((n, RMAX, 2 * sources), bf16)
    xt_like = jax.ShapeDtypeStruct((2 * sources, model_rows), f32)

    def call(kernel, out_shape, *args):
        return pl.pallas_call(
            kernel,
            out_shape=out_shape,
            in_specs=[scalars] + [on_chip] * (len(args) - 1),
            out_specs=jax.tree.map(lambda _: on_chip, out_shape),
            scratch_shapes=rows,
            compiler_params=pltpu.CompilerParams(vmem_limit_bytes=VMEM_GRANT),
            cost_estimate=pl.CostEstimate(
                flops=16 * total * model_rows * sources,
                bytes_accessed=4 * total * model_rows,
                transcendentals=0,
            ),
        )(*args)

    xt, outbound = call(first_kernel, (xt_like, slots_like), ranks, start_model, v_basis)
    sums = window_sums(records, window_start, window_stop)
    for iteration in range(ITERS):
        arrived = exchange(outbound)
        outgoing = call(data_kernel, slots_like, ranks, arrived, u_parts, sums)
        returned = exchange(outgoing)
        if iteration + 1 < ITERS:
            xt, outbound = call(model_kernel, (xt_like, slots_like), ranks, returned, v_basis, xt)
    final_like = jax.ShapeDtypeStruct(start_model.shape, f32)
    return call(last_kernel, final_like, ranks, returned, v_basis, xt)


def solution(mesh):
    in_specs = (
        P(None, ("groups", "tile"), None),
        P(None, ("groups", "tile"), None),
        P(None, None, None, ("groups", "tile")),
        P(None, None, ("groups", "tile")),
        P("groups", None, None),
        P(None, ("groups", "tile")),
        P(None, ("groups", "tile")),
    )
    out_specs = P(None, ("groups", "tile"), None)
    return jax.shard_map(
        on_device, mesh=mesh, in_specs=in_specs, out_specs=out_specs, check_vma=False
    )
```
